256 devices in a mesh: sub: 32 (over z, x), agg: 8 (over y, core).
Axes of the slice: x: 4, y: 4, z: 8, core: 2. Of those that a mesh axis runs over, the one named last changes fastest.
Arguments:
- dual_load: float32 [8, 32, 64, 1536], P('agg', 'sub'), may hold values from -58 to 58
- interface_inverse: bfloat16 [8, 32, 1536, 1536], P('agg', 'sub'), may hold values from -1 to 2.5, as said below
- dirichlet: bfloat16 [8, 32, 1536, 1536], P('agg', 'sub'), may hold values from -1 to 2.5, as said below
- coupling: bfloat16 [8, 32, 128, 1536], P('agg', 'sub'), may hold values from -0.15625 to 0.15625
- neighbours: int32 [8, 32, 8], P('agg', 'sub'), may hold values from -1 to 31, as said below
- face_counts: int32 [8, 32, 8], P('agg', 'sub'), may hold values from 0 to 192, as said below
- owners: int32 [8, 32, 128, 1], P('agg', 'sub'), may hold values from 0 to 7; in each aligned block of 128 rows (0 to 127, 128 to 255, ..., all dimensions but the last counted through in order) at most 48 rows name the same one
- primal_rows: int32 [8, 32, 128], P('agg', 'sub'), may hold values from 0 to 1023
- coarse_inverse: float32 [8, 1024, 1024], P('agg', 'sub'), may hold values from -1 to 1.5, as said below
Outputs:
- solution: float32 [8, 32, 64, 1536], P('agg', 'sub')
- residual: float32 [8, 32, 64, 1536], P('agg', 'sub')
The draws below stay inside these ranges and needn't reach their ends.
Inputs may be any that keep to these rules, and one draw needn't show every extreme that they name: `neighbours`: each subdomain lists peers of its own aggregate by their index along sub, -1 in empty slots; no peer twice; if j lists i then i lists j; every listed peer lies within a cyclic distance of 4 along sub. `face_counts`: 0 exactly in empty slots, 48 or more elsewhere; both sides of a face give the same count and hold its rows in the same order. `owners`: among the 128 primal rows of one subdomain no aggregate is named more than 48 times. `interface_inverse`: each subdomain's matrix is symmetric positive definite. `dirichlet`: each subdomain's matrix is symmetric positive definite. `coarse_inverse`: each aggregate's matrix is symmetric positive definite.
All inputs are finite; a program needn't handle non-finite values.
Results may differ from the reference program's by a relative error of at most 0.011.
Values sent between devices are 32-bit elements; how exact they have to be, the bound alone decides.
No kernel may reach another device: no remote copies, remote signals or barrier semaphores. Data moves between devices by JAX's collectives and lax.ppermute only.
A program may use at most 128 MiB of HBM per device.

```python
import math
import jax
import jax.numpy as jnp
import numpy as np
from jax import lax

NB = 8
FMAX = 192
NI = 1536
NRHS = 64
NP = 128
NC = 1024
CAP = 48
ITERS = 2
REACH = 4
N_SUB = 32
N_AGG = 8


def spd_block(key, order, lowest, highest, spread):
    first, second = jax.random.split(key)
    noise = jnp.clip(jax.random.normal(first, (order, order), jnp.float32), -4.0, 4.0)
    diagonal = jax.random.uniform(second, (order,), jnp.float32, lowest, highest)
    symmetric = (noise + noise.T) * (spread / math.sqrt(2.0 * order))
    return symmetric + jnp.diag(diagonal)


def draw_interface_inverse(key, part):

    def single(index):
        return spd_block(jax.random.fold_in(jax.random.fold_in(key, 11), index), NI, 1.0, 2.0, 0.4).astype(jnp.bfloat16)
    blocks = lax.map(single, jnp.arange(N_AGG * N_SUB, dtype=jnp.int32))
    return blocks.reshape(N_AGG, N_SUB, NI, NI)


def draw_dirichlet(key, part):

    def single(index):
        return spd_block(jax.random.fold_in(jax.random.fold_in(key, 23), index), NI, 1.0, 2.0, 0.35).astype(jnp.bfloat16)
    blocks = lax.map(single, jnp.arange(N_AGG * N_SUB, dtype=jnp.int32))
    return blocks.reshape(N_AGG, N_SUB, NI, NI)


def draw_coarse_inverse(key, part):

    def single(index):
        return spd_block(jax.random.fold_in(jax.random.fold_in(key, 37), index), NC, 0.5, 1.0, 0.2)
    return lax.map(single, jnp.arange(N_AGG, dtype=jnp.int32))


def draw_dual_load(key, part):
    first, second, third = jax.random.split(jax.random.fold_in(key, 5), 3)
    shape = (N_AGG, N_SUB, NRHS, NI)
    base = jnp.clip(jax.random.normal(first, shape, jnp.float32), -3.0, 3.0)
    row_scale = jnp.exp(jax.random.uniform(second, (1, 1, 1, NI), jnp.float32, -1.15, 1.15))
    case_scale = jnp.exp(jax.random.uniform(third, (1, 1, NRHS, 1), jnp.float32, -0.7, 0.7))
    place = jnp.arange(N_AGG * N_SUB, dtype=jnp.float32).reshape(N_AGG, N_SUB, 1, 1) / max(N_AGG * N_SUB - 1, 1)
    rising = jnp.exp(math.log(3.0) * place)
    return base * row_scale * case_scale * rising


def face_graph(key):
    first, second = jax.random.split(jax.random.fold_in(key, 77))
    keep = jax.random.randint(first, (N_AGG, REACH, N_SUB), 0, 5) < 4
    sizes = jax.random.randint(second, (N_AGG, REACH, N_SUB), FMAX // 4, FMAX + 1)
    keep = keep.at[:, 0, 0].set(True)
    keep = keep.at[:, REACH - 1, 1].set(False)
    sizes = sizes.at[:, 0, 0].set(FMAX)
    peers = jnp.arange(N_SUB, dtype=jnp.int32)[None, :]
    lists = []
    counts = []
    for offset in range(REACH):
        distance = offset + 1
        lists.append(jnp.where(keep[:, offset], (peers + distance) % N_SUB, -1))
        counts.append(jnp.where(keep[:, offset], sizes[:, offset], 0))
        back_keep = jnp.roll(keep[:, offset], distance, axis=1)
        back_size = jnp.roll(sizes[:, offset], distance, axis=1)
        lists.append(jnp.where(back_keep, (peers + N_SUB - distance) % N_SUB, -1))
        counts.append(jnp.where(back_keep, back_size, 0))
    for filler in range(NB - 2 * REACH):
        lists.append(jnp.full((N_AGG, N_SUB), -1, jnp.int32))
        counts.append(jnp.zeros((N_AGG, N_SUB), jnp.int32))
    return (jnp.stack(lists, axis=-1).astype(jnp.int32), jnp.stack(counts, axis=-1).astype(jnp.int32))


def draw_neighbours(key, part):
    return face_graph(key)[0]


def draw_face_counts(key, part):
    return face_graph(key)[1]


def set_ends(drawn, key, low, top_value):
    extent = drawn.shape
    index_at = [jax.random.randint(jax.random.fold_in(key, axis), (), 0, extent[axis]) for axis in range(len(extent))]
    drawn = drawn.at[tuple(index_at)].set(low)
    longest = extent.index(max(extent))
    index_at[longest] = (index_at[longest] + 1) % extent[longest]
    return drawn.at[tuple(index_at)].set(top_value)


def levels(rng, dims, cuts, least, top_value):
    def one(position, parts):
        draws = jax.random.uniform(jax.random.fold_in(jax.random.fold_in(rng, 6), position), (parts,), jnp.float32, least / len(cuts), top_value / len(cuts))
        return jnp.repeat(jnp.exp(draws), dims[position] // parts).reshape((-1,) + (1,) * (len(dims) - position - 1))

    factor_of = one(*cuts[0])
    for cut in cuts[1:]:
        factor_of = factor_of * one(*cut)
    return factor_of


def deal_out(rng, own, number, rows, count, top, limit, slope):
    sequence = jax.random.permutation(rng, count)
    heavy_load, ordinary = load_shares(count, rows * top, limit, slope, True), load_shares(count, rows * top, limit, slope, False)
    places = jnp.arange(count)

    def named(lengths, turn):
        used = int((lengths > 0).sum())
        fixed = max(1, used // 4)
        passed = fixed + (places - fixed + turn * (used - fixed)) % max(1, count - fixed)
        return jnp.zeros((count,), jnp.int32).at[sequence[jnp.where(places < fixed, places, passed)]].set(jnp.asarray(lengths, jnp.int32))

    lengths = jnp.where(number % 4 == 0, named(heavy_load, number // 4), named(ordinary, number - number // 4 - 1))
    mixed = jax.random.permutation(jax.random.fold_in(own, 3), count)
    giver, sink = mixed[0:count // 2 * 2:2], mixed[1:count // 2 * 2:2]
    room = jnp.minimum(lengths[giver] - 1, limit - lengths[sink]) // 2
    room = jnp.where((giver == sequence[0]) | (sink == sequence[0]) | (lengths[sink] == 0), 0, jnp.maximum(room, 0))
    passed = jax.random.randint(jax.random.fold_in(own, 4), (count // 2,), 0, 1 << 20) % (room + 1)
    lengths = lengths.at[giver].add(-passed).at[sink].add(passed)
    items = jnp.searchsorted(jnp.cumsum(lengths), jnp.arange(rows * top), side="right").astype(jnp.int32)
    table = items.reshape(top, rows).T
    table = table[jax.random.permutation(jax.random.fold_in(own, 1), rows)]
    turn = jax.random.randint(jax.random.fold_in(own, 2), (rows, 1), 0, top)
    return jnp.take_along_axis(table, (jnp.arange(top)[None, :] + turn) % top, axis=1)


def load_shares(amount, total, limit, lean, full):
    portions = [(1 << 20) // math.isqrt(standing ** lean) + 1 for standing in range(1, amount + 1)]
    largest = limit if full else min(limit, max(-(-total // amount), total * portions[0] // sum(portions)))
    least = 1 if total - largest >= amount - 1 else 0
    given, surplus = [largest] + [least] * (amount - 1), total - largest - least * (amount - 1)
    while surplus > 0:
        free = [i for i in range(1, amount) if given[i] < largest] or [i for i in range(1, amount) if given[i] < limit]
        whole, budget = sum([portions[i] for i in free]), surplus
        for i in free:
            addition = min(limit - given[i], max(1, budget * portions[i] // whole), surplus)
            given[i] = given[i] + addition
            surplus = surplus - addition
    return np.array(given)


def bell_draw(stream_key, shape, scale, most, cuts=(), kind=jnp.bfloat16):
    result = jax.random.normal(stream_key, shape, jnp.float32) * scale
    if len(cuts) > 0:
        result = levels(stream_key, shape, cuts, -0.22, 0.18) * result
    return jnp.clip(result, min=-most, max=most).astype(kind)


def setup_inputs(seed: int = 0) -> dict:
    key_list = jax.random.split(jax.random.key(seed), 10)
    dual_load = draw_dual_load(jax.random.fold_in(key_list[9], 71), 0)
    interface_inverse = draw_interface_inverse(jax.random.fold_in(key_list[9], 71), 0)
    dirichlet = draw_dirichlet(jax.random.fold_in(key_list[9], 71), 0)
    coupling = bell_draw(key_list[3], (N_AGG, N_SUB, NP, NI), NI ** -0.5, 0.15625, ((0, 8), (1, 32)))
    neighbours = draw_neighbours(jax.random.fold_in(key_list[9], 71), 0)
    face_counts = draw_face_counts(jax.random.fold_in(key_list[9], 71), 0)
    owners_keys = jax.random.split(jax.random.fold_in(key_list[6], 1), N_AGG * N_SUB * NP // NP)
    owners_turns = jax.random.permutation(jax.random.fold_in(key_list[6], 3), N_AGG * N_SUB * NP // NP)
    owners = jax.vmap(lambda own, number: deal_out(jax.random.fold_in(key_list[6], 2), own, number, NP, N_AGG, 1, CAP, 2))(owners_keys, owners_turns).reshape((N_AGG, N_SUB, NP, 1))
    primal_rows = set_ends(jax.random.randint(key_list[7], (N_AGG, N_SUB, NP), 0, NC), jax.random.fold_in(key_list[7], 1), 0, NC - 1).astype(jnp.int32)
    coarse_inverse = draw_coarse_inverse(jax.random.fold_in(key_list[9], 71), 0)
    return {"dual_load": dual_load, "interface_inverse": interface_inverse, "dirichlet": dirichlet, "coupling": coupling, "neighbours": neighbours, "face_counts": face_counts, "owners": owners, "primal_rows": primal_rows, "coarse_inverse": coarse_inverse}


FULL_PRECISION = lax.Precision.HIGHEST
CONTRACT_LAST = (((1,), (1,)), ((), ()))


def row_mask(face_counts):
    depth = jnp.arange(FMAX, dtype=jnp.int32)
    inside = depth[None, None, None, :] < face_counts[:, :, :, None]
    return inside.reshape(N_AGG, N_SUB, 1, NI).astype(jnp.float32)


def link_table(neighbours):
    peers = jnp.arange(N_SUB, dtype=jnp.int32)
    goes = neighbours[:, :, :, None] == peers[None, None, None, :]
    back = jnp.transpose(goes, (0, 3, 1, 2))
    table = goes[:, :, :, :, None] & back[:, :, None, :, :]
    return table.astype(jnp.float32)


def assemble(local, links, mask):
    faces = local.reshape(N_AGG, N_SUB, NRHS, NB, FMAX)

    def per_aggregate(operands):
        return jnp.einsum("ikjl,jrlf->irkf", operands[1], operands[0], precision=FULL_PRECISION)

    incoming = lax.map(per_aggregate, (faces, links))
    return mask * (local + incoming.reshape(local.shape))


def batched_dot(left, right):
    return lax.map(lambda operands: jnp.dot(operands[0], operands[1], preferred_element_type=jnp.float32), (left, right))


def coarse_values(terms, owners, primal_rows, coarse_inverse):
    target = (owners.reshape(-1) * NC + primal_rows.reshape(-1)).astype(jnp.int32)
    columns = jnp.transpose(terms, (0, 2, 1)).reshape(-1, NRHS)
    summed = jax.ops.segment_sum(columns, target, num_segments=N_AGG * NC).reshape(N_AGG, NC, NRHS)
    solved = jnp.einsum("acd,adr->acr", coarse_inverse, summed, precision=FULL_PRECISION)
    picked = solved.reshape(N_AGG * NC, NRHS)[target]
    return jnp.transpose(picked.reshape(-1, NP, NRHS), (0, 2, 1))


def reference(dual_load, interface_inverse, dirichlet, coupling, neighbours, face_counts, owners, primal_rows, coarse_inverse):
    mask = row_mask(face_counts)
    links = link_table(neighbours)
    inverse_flat = interface_inverse.reshape(-1, NI, NI)
    dirichlet_flat = dirichlet.reshape(-1, NI, NI)
    coupling_flat = coupling.reshape(-1, NP, NI)

    def operator(field):
        packed = field.reshape(-1, NRHS, NI).astype(jnp.bfloat16)
        own = batched_dot(packed, inverse_flat)
        terms = lax.map(lambda operands: lax.dot_general(operands[0], operands[1], CONTRACT_LAST, preferred_element_type=jnp.float32), (packed, coupling_flat))
        local_back = coarse_values(terms, owners, primal_rows, coarse_inverse).astype(jnp.bfloat16)
        correction = batched_dot(local_back, coupling_flat)
        local = mask * (own + correction).reshape(N_AGG, N_SUB, NRHS, NI)
        return assemble(local, links, mask)

    def precondition(field):
        packed = field.reshape(-1, NRHS, NI).astype(jnp.bfloat16)
        local = mask * batched_dot(packed, dirichlet_flat).reshape(N_AGG, N_SUB, NRHS, NI)
        return assemble(local, links, mask)

    def inner(first, second):
        return jnp.sum(first * second, axis=(0, 1, 3))

    rhs = assemble(mask * dual_load, links, mask)
    solution = jnp.zeros_like(rhs)
    residual = rhs
    precond = precondition(residual)
    direction = precond
    residual_dot = inner(residual, precond)
    for iteration in range(ITERS):
        image = operator(direction)
        alpha = (residual_dot / inner(direction, image))[None, None, :, None]
        solution = solution + alpha * direction
        residual = residual - alpha * image
        if iteration + 1 < ITERS:
            precond = precondition(residual)
            next_dot = inner(residual, precond)
            direction = precond + (next_dot / residual_dot)[None, None, :, None] * direction
            residual_dot = next_dot
    return solution, residual
```

```python
import functools

import jax
import jax.numpy as jnp
from jax import lax
from jax.experimental import pallas as pl
from jax.experimental.pallas import tpu as pltpu
from jax.sharding import PartitionSpec as P

NB = 8
FMAX = 192
NI = 1536
NRHS = 64
NP = 128
NC = 1024
CAP = 48
N_SUB = 32
N_AGG = 8
N_DEV = N_SUB * N_AGG
HALF = 64
LANES = 128
PACKED = N_AGG * HALF
CHUNK = 2 * FMAX
N_CHUNK = NI // CHUNK
HI = NC // LANES
DOT_RZ, DOT_OWN, DOT_CROSS, DOT_COARSE = CAP, CAP + 1, CAP + 2, CAP + 3
F32 = jnp.float32
BF16 = jnp.bfloat16
I32 = jnp.int32
LANES_BOTH = (((1,), (1,)), ((), ()))
VMEM = pl.BlockSpec(memory_space=pltpu.VMEM)
SMEM = pl.BlockSpec(memory_space=pltpu.SMEM)
ANY = pl.BlockSpec(memory_space=pl.ANY)
FACE = jax.ShapeDtypeStruct((NRHS, FMAX), F32)
FIELD = jax.ShapeDtypeStruct((NRHS, NI), F32)


def slot_direction(nbr_ref, pos_ref, slot):
    peer = nbr_ref[slot]
    ahead = lax.rem(peer - pos_ref[0] + N_SUB, N_SUB)
    index = jnp.where(ahead <= NB // 2, 2 * (ahead - 1), 2 * (N_SUB - 1 - ahead) + 1)
    return jnp.where(peer < 0, NB, index)


def inside(cnt_ref, slot):
    depth = lax.broadcasted_iota(I32, (NRHS, FMAX), 1)
    return depth < cnt_ref[slot]


def face(slot):
    return slice(slot * FMAX, (slot + 1) * FMAX)


def send_faces(buffer, out_refs):
    for direction in range(NB):
        out_refs[direction][...] = buffer[direction]


def clear(buffer):
    for direction in range(NB):
        buffer[direction] = jnp.zeros((NRHS, FMAX), F32)


def take_faces(buffer, in_refs):
    for direction in range(NB):
        buffer[direction] = in_refs[direction][...]


def received(buffer, nbr_ref, pos_ref, slot):
    direction = slot_direction(nbr_ref, pos_ref, slot)
    return buffer[jnp.where(direction == NB, 0, lax.bitwise_xor(direction, 1))]


def assembled(local_ref, buffer, nbr_ref, cnt_ref, pos_ref, slot):
    total = local_ref[:, face(slot)] + received(buffer, nbr_ref, pos_ref, slot)
    return jnp.where(inside(cnt_ref, slot), total, 0.0)


def start_matrix(matrix_hbm, chunks, sems):
    copies = []
    for part in range(N_CHUNK):
        copy = pltpu.make_async_copy(
            matrix_hbm.at[:, pl.ds(part * CHUNK, CHUNK)], chunks.at[part], sems.at[part]
        )
        copy.start()
        copies.append(copy)
    return copies


def row_sum(value):
    return jnp.sum(value, axis=1, keepdims=True)


def setup_kernel(
    nbr_ref,
    cnt_ref,
    pos_ref,
    load_ref,
    owner_col,
    owner_row,
    row_col,
    coupling_ref,
    *rest,
):
    outs, packed_ref, ids_ref, buffer = rest[:NB], rest[NB], rest[NB + 1], rest[NB + 2]
    clear(buffer)
    for slot in range(NB):
        value = jnp.where(inside(cnt_ref, slot), load_ref[:, face(slot)], 0.0)
        buffer[slot_direction(nbr_ref, pos_ref, slot)] = value
    send_faces(buffer, outs)
    same = owner_col[...] == owner_row[...]
    down = lax.broadcasted_iota(I32, (NP, NP), 0)
    across = lax.broadcasted_iota(I32, (NP, NP), 1)
    rank_row = jnp.sum(jnp.where(same & (down < across), 1.0, 0.0), axis=0, keepdims=True)
    rank_col = row_sum(jnp.where(same & (across < down), 1.0, 0.0))
    slot_row = owner_row[...] * HALF + rank_row.astype(I32)
    slot_col = owner_col[...] * HALF + rank_col.astype(I32)
    packing = jnp.where(lax.broadcasted_iota(I32, (PACKED, NP), 0) == slot_row, 1.0, 0.0)
    packed_ref[...] = jnp.dot(
        packing.astype(BF16), coupling_ref[...], preferred_element_type=F32
    ).astype(BF16)
    hit = lax.broadcasted_iota(I32, (NP, PACKED), 1) == slot_col
    named = jnp.where(hit, (row_col[...] + 1).astype(F32), 0.0)
    ids_ref[...] = jnp.sum(named, axis=0, keepdims=True) - 1.0


def smooth(field_bf, copies, chunks, nbr_ref, cnt_ref, pos_ref, local_ref, buffer):
    for part in range(N_CHUNK):
        copies[part].wait()
        product = jnp.dot(field_bf[...], chunks[part], preferred_element_type=F32)
        for side in range(2):
            slot = 2 * part + side
            value = jnp.where(inside(cnt_ref, slot), product[:, face(side)], 0.0)
            local_ref[:, face(slot)] = value
            buffer[slot_direction(nbr_ref, pos_ref, slot)] = value


def first_precond_kernel(nbr_ref, cnt_ref, pos_ref, load_ref, matrix_hbm, *rest):
    ins, outs = rest[:NB], rest[NB : 2 * NB]
    residual_ref, local_ref, buffer, field_bf, chunks, sems = rest[2 * NB :]
    copies = start_matrix(matrix_hbm, chunks, sems)
    take_faces(buffer, ins)
    for slot in range(NB):
        value = assembled(load_ref, buffer, nbr_ref, cnt_ref, pos_ref, slot)
        residual_ref[:, face(slot)] = value
        field_bf[:, face(slot)] = value.astype(BF16)
    clear(buffer)
    smooth(field_bf, copies, chunks, nbr_ref, cnt_ref, pos_ref, local_ref, buffer)
    send_faces(buffer, outs)


def next_precond_kernel(
    nbr_ref, cnt_ref, pos_ref, image_ref, residual_in, scalars_ref, matrix_hbm, *rest
):
    ins, outs = rest[:NB], rest[NB : 2 * NB]
    full_ref, residual_ref, local_ref, buffer, field_bf, chunks, sems = rest[2 * NB :]
    copies = start_matrix(matrix_hbm, chunks, sems)
    take_faces(buffer, ins)
    alpha = scalars_ref[:, 0:1]
    for slot in range(NB):
        value = assembled(image_ref, buffer, nbr_ref, cnt_ref, pos_ref, slot)
        full_ref[:, face(slot)] = value
        value = residual_in[:, face(slot)] - alpha * value
        residual_ref[:, face(slot)] = value
        field_bf[:, face(slot)] = value.astype(BF16)
    clear(buffer)
    smooth(field_bf, copies, chunks, nbr_ref, cnt_ref, pos_ref, local_ref, buffer)
    send_faces(buffer, outs)


def operator_kernel(first, nbr_ref, cnt_ref, pos_ref, local_ref, residual_ref, *rest):
    rest = list(rest)
    image_ref = None if first else rest.pop(0)
    packed_ref, ids_ref, matrix_hbm = rest[:3]
    ins = rest[3 : 3 + NB]
    field_ref, own_ref, send_ref, buffer, field_bf, chunks, sems = rest[3 + NB :]
    copies = start_matrix(matrix_hbm, chunks, sems)
    take_faces(buffer, ins)
    for slot in range(NB):
        value = assembled(local_ref, buffer, nbr_ref, cnt_ref, pos_ref, slot)
        field_ref[:, face(slot)] = value
        field_bf[:, face(slot)] = value.astype(BF16)
    terms = lax.dot_general(
        field_bf[...], packed_ref[...], LANES_BOTH, preferred_element_type=F32
    )
    for part in range(N_CHUNK):
        copies[part].wait()
        own_ref[:, part * CHUNK : (part + 1) * CHUNK] = jnp.dot(
            field_bf[...], chunks[part], preferred_element_type=F32
        )
    field = field_ref[...]
    rz = row_sum(residual_ref[...] * field)
    own_dot = row_sum(field * own_ref[...])
    place = lax.bitwise_and(lax.broadcasted_iota(I32, (NRHS, PACKED), 1), HALF - 1)
    terms = jnp.where(place == DOT_RZ, rz, terms)
    terms = jnp.where(place == DOT_OWN, own_dot, terms)
    if not first:
        terms = jnp.where(place == DOT_CROSS, row_sum(field * image_ref[...]), terms)
    for owner in range(N_AGG):
        piece = terms[:, owner * HALF : (owner + 1) * HALF]
        message = jnp.concatenate([piece[:N_SUB], piece[N_SUB:]], axis=1)
        if first:
            send_ref[pl.ds(2 * owner * N_SUB, N_SUB, stride=2), :] = message
            named = ids_ref[:, owner * HALF : (owner + 1) * HALF]
            named = jnp.broadcast_to(jnp.concatenate([named, named], axis=1), (N_SUB, LANES))
            send_ref[pl.ds(2 * owner * N_SUB + 1, N_SUB, stride=2), :] = named
        else:
            send_ref[owner * N_SUB : (owner + 1) * N_SUB, :] = message


def split3(value):
    high = value.astype(BF16).astype(F32)
    rest = value - high
    middle = rest.astype(BF16).astype(F32)
    return high, middle, rest - middle


def coarse_kernel(first, got_ref, inverse_ref, *rest):
    if first:
        send_ref, low_ref, high_ref, parts, answer, values = rest
        values[...] = got_ref[pl.ds(0, N_DEV, stride=2), :].T
        named = got_ref[pl.ds(1, N_DEV, stride=2), :].T.astype(I32)
        high_ref[...] = lax.shift_right_arithmetic(named[:HALF], 7)
        low_rows = lax.bitwise_and(named[:HALF], LANES - 1)
        down = lax.broadcasted_iota(I32, (LANES, N_DEV), 0)
        for j in range(CAP):
            low_ref[:, j * N_DEV : (j + 1) * N_DEV] = jnp.where(
                down == low_rows[j : j + 1], 1.0, 0.0
            ).astype(BF16)
    else:
        low_ref, high_ref, send_ref, parts, answer, values = rest
        values[...] = got_ref[...].T
    for index, part in enumerate(split3(values[...])):
        parts[index] = part
    up = lax.broadcasted_iota(I32, (HI, N_DEV), 0)
    gathered = jnp.zeros((LANES, 6 * HI), F32)
    for j in range(CAP):
        hit = up == high_ref[j : j + 1, :]
        spread = [
            jnp.where(hit, parts[part, case * HALF + j : case * HALF + j + 1, :], 0.0)
            for part in range(3)
            for case in range(2)
        ]
        gathered += lax.dot_general(
            low_ref[:, j * N_DEV : (j + 1) * N_DEV],
            jnp.concatenate(spread, axis=0).astype(BF16),
            LANES_BOTH,
            preferred_element_type=F32,
        )
    width = 2 * HI
    rhs = gathered[:, :width] + gathered[:, width : 2 * width] + gathered[:, 2 * width :]
    rows = []
    for case in range(2):
        total = jnp.zeros((1, NC), F32)
        for high in range(HI):
            column = rhs[:, case * HI + high : case * HI + high + 1]
            block = inverse_ref[high * LANES : (high + 1) * LANES, :]
            total += jnp.sum(block * column, axis=0, keepdims=True)
        rows += [total[:, high * LANES : (high + 1) * LANES] for high in range(HI)]
    stacked = jnp.concatenate(split3(jnp.concatenate(rows, axis=0)), axis=0).astype(BF16)
    for j in range(CAP):
        hit = up == high_ref[j : j + 1, :]
        picked = jnp.dot(
            stacked, low_ref[:, j * N_DEV : (j + 1) * N_DEV], preferred_element_type=F32
        )
        picked = picked[:width] + picked[width : 2 * width] + picked[2 * width :]
        for case in range(2):
            mine = jnp.where(hit, picked[case * HI : (case + 1) * HI], 0.0)
            answer[case * HALF + j : case * HALF + j + 1, :] = jnp.sum(
                mine, axis=0, keepdims=True
            )
    totals = jnp.broadcast_to(row_sum(values[...]), (LANES, N_DEV))
    for case in range(2):
        rows = slice(case * HALF, case * HALF + CAP)
        answer[case * HALF + CAP : (case + 1) * HALF, :] = totals[
            case * HALF + CAP : (case + 1) * HALF
        ]
        both = row_sum(values[rows, :] * answer[rows, :])
        answer[case * HALF + DOT_COARSE : case * HALF + DOT_COARSE + 1, :] = jnp.broadcast_to(
            jnp.sum(both, axis=0, keepdims=True), (1, N_DEV)
        )
    send_ref[...] = answer[...].T


def correct_kernel(first, nbr_ref, cnt_ref, pos_ref, got_ref, packed_ref, own_ref, *rest):
    rest = list(rest)
    before_ref = None if first else rest.pop(0)
    local_ref, scalars_ref = rest[:2]
    outs = rest[2 : 2 + NB]
    buffer, back = rest[2 + NB :]
    for owner in range(N_AGG):
        block = got_ref[owner * N_SUB : (owner + 1) * N_SUB, :]
        back[:, owner * HALF : (owner + 1) * HALF] = jnp.concatenate(
            [block[:, :HALF], block[:, HALF:]], axis=0
        )
    correction = jnp.dot(back[...].astype(BF16), packed_ref[...], preferred_element_type=F32)
    clear(buffer)
    for slot in range(NB):
        value = own_ref[:, face(slot)] + correction[:, face(slot)]
        value = jnp.where(inside(cnt_ref, slot), value, 0.0)
        local_ref[:, face(slot)] = value
        buffer[slot_direction(nbr_ref, pos_ref, slot)] = value
    send_faces(buffer, outs)
    coarse = back[:, DOT_COARSE : DOT_COARSE + 1]
    for owner in range(1, N_AGG):
        at = owner * HALF + DOT_COARSE
        coarse = coarse + back[:, at : at + 1]
    rz = back[:, DOT_RZ : DOT_RZ + 1]
    energy = 2.0 * (back[:, DOT_OWN : DOT_OWN + 1] + coarse)
    lane = lax.broadcasted_iota(I32, (NRHS, LANES), 1)
    if first:
        columns = (rz / energy, rz, energy)
    else:
        beta = rz / before_ref[:, 1:2]
        cross = back[:, DOT_CROSS : DOT_CROSS + 1]
        energy = energy + 2.0 * beta * cross + beta * beta * before_ref[:, 2:3]
        columns = (rz / energy, beta, before_ref[:, 0:1])
    scalars = jnp.zeros((NRHS, LANES), F32)
    for index, column in enumerate(columns):
        scalars = jnp.where(lane == index, column, scalars)
    scalars_ref[...] = scalars


def final_kernel(
    nbr_ref,
    cnt_ref,
    pos_ref,
    local_ref,
    image_ref,
    residual_in,
    field0_ref,
    field1_ref,
    scalars_ref,
    *rest,
):
    ins = rest[:NB]
    solution_ref, residual_ref, buffer = rest[NB:]
    take_faces(buffer, ins)
    alpha, beta = scalars_ref[:, 0:1], scalars_ref[:, 1:2]
    alpha_before = scalars_ref[:, 2:3]
    for slot in range(NB):
        value = assembled(local_ref, buffer, nbr_ref, cnt_ref, pos_ref, slot)
        value = value + beta * image_ref[:, face(slot)]
        residual_ref[:, face(slot)] = residual_in[:, face(slot)] - alpha * value
    before = field0_ref[...]
    solution_ref[...] = alpha_before * before + alpha * (field1_ref[...] + beta * before)


def exchange(blocks):
    moved = []
    for direction, block in enumerate(blocks):
        step = (direction // 2 + 1) * (1 if direction % 2 == 0 else -1)
        route = [(i, (i + step) % N_SUB) for i in range(N_SUB)]
        moved.append(lax.ppermute(block, "sub", route))
    return moved


FACES = pltpu.VMEM((NB + 1, NRHS, FMAX), F32)
MATRIX = [
    pltpu.VMEM((NRHS, NI), BF16),
    pltpu.VMEM((N_CHUNK, NI, CHUNK), BF16),
    pltpu.SemaphoreType.DMA((N_CHUNK,)),
]
PARAMS = pltpu.CompilerParams(vmem_limit_bytes=40 << 20)


def call(kernel, outs, in_specs, scratch):
    return pl.pallas_call(
        kernel,
        out_shape=outs,
        in_specs=in_specs,
        out_specs=[VMEM] * len(outs),
        scratch_shapes=scratch,
        compiler_params=PARAMS,
    )


def shards(
    dual_load,
    interface_inverse,
    dirichlet,
    coupling,
    neighbours,
    face_counts,
    owners,
    primal_rows,
    coarse_inverse,
):
    load = dual_load[0, 0]
    stiffness, dirichlet_block = interface_inverse[0, 0], dirichlet[0, 0]
    graph = (neighbours[0, 0], face_counts[0, 0], lax.axis_index("sub").astype(I32)[None])
    inverse = lax.all_gather(coarse_inverse[0], "sub", axis=0, tiled=True)
    owner_col = owners[0, 0]
    packed_shape = jax.ShapeDtypeStruct((PACKED, NI), BF16)
    *faces, packed, ids = call(
        setup_kernel,
        [FACE] * NB + [packed_shape, jax.ShapeDtypeStruct((1, PACKED), F32)],
        [SMEM] * 3 + [VMEM] * 5,
        [FACES],
    )(
        *graph,
        load,
        owner_col,
        owner_col.reshape(1, NP),
        primal_rows[0, 0].reshape(NP, 1),
        coupling[0, 0],
    )
    faces = exchange(faces)
    *faces, residual, local = call(
        first_precond_kernel,
        [FACE] * NB + [FIELD, FIELD],
        [SMEM] * 3 + [VMEM, ANY] + [VMEM] * NB,
        [FACES] + MATRIX,
    )(*graph, load, dirichlet_block, *faces)
    message = jax.ShapeDtypeStruct((N_DEV, LANES), F32)
    low_shape = jax.ShapeDtypeStruct((LANES, CAP * N_DEV), BF16)
    high_shape = jax.ShapeDtypeStruct((HALF, N_DEV), I32)
    coarse_scratch = [
        pltpu.VMEM((3, LANES, N_DEV), F32),
        pltpu.VMEM((LANES, N_DEV), F32),
        pltpu.VMEM((LANES, N_DEV), F32),
    ]
    axes = ("agg", "sub")
    keep = []
    low = high = scalars = image = field0 = None
    for step in range(2):
        first = step == 0
        faces = exchange(faces)
        extra = [] if first else [image]
        send_shape = jax.ShapeDtypeStruct((2 * N_DEV if first else N_DEV, LANES), F32)
        field, own, send = call(
            functools.partial(operator_kernel, first),
            [FIELD, FIELD, send_shape],
            [SMEM] * 3 + [VMEM] * (2 + len(extra)) + [VMEM, VMEM, ANY] + [VMEM] * NB,
            [FACES] + MATRIX,
        )(*graph, local, residual, *extra, packed, ids, stiffness, *faces)
        pieces = 2 if first else 1
        got = lax.all_to_all(
            send.reshape(N_DEV, pieces, LANES), axes, split_axis=0, concat_axis=0, tiled=True
        ).reshape(N_DEV * pieces, LANES)
        if first:
            answer, low, high = call(
                functools.partial(coarse_kernel, True),
                [message, low_shape, high_shape],
                [VMEM, VMEM],
                coarse_scratch,
            )(got, inverse)
        else:
            (answer,) = call(
                functools.partial(coarse_kernel, False),
                [message],
                [VMEM] * 4,
                coarse_scratch,
            )(got, inverse, low, high)
        got = lax.all_to_all(
            answer.reshape(N_DEV, 1, LANES), axes, split_axis=0, concat_axis=0, tiled=True
        ).reshape(N_DEV, LANES)
        extra = [] if first else [scalars]
        local, scalars, *faces = call(
            functools.partial(correct_kernel, first),
            [FIELD, jax.ShapeDtypeStruct((NRHS, LANES), F32)] + [FACE] * NB,
            [SMEM] * 3 + [VMEM] * (3 + len(extra)),
            [FACES, pltpu.VMEM((NRHS, PACKED), F32)],
        )(*graph, got, packed, own, *extra)
        faces = exchange(faces)
        if first:
            field0 = field
            *faces, image, residual, local = call(
                next_precond_kernel,
                [FACE] * NB + [FIELD] * 3,
                [SMEM] * 3 + [VMEM] * 3 + [ANY] + [VMEM] * NB,
                [FACES] + MATRIX,
            )(*graph, local, residual, scalars, dirichlet_block, *faces)
    solution_out, residual_out = call(
        final_kernel,
        [FIELD, FIELD],
        [SMEM] * 3 + [VMEM] * 6 + [VMEM] * NB,
        [FACES],
    )(*graph, local, image, residual, field0, field, scalars, *faces)
    return (solution_out[None, None], residual_out[None, None])


def solution(mesh):
    in_specs = (
        P("agg", "sub", None, None),
        P("agg", "sub", None, None),
        P("agg", "sub", None, None),
        P("agg", "sub", None, None),
        P("agg", "sub", None),
        P("agg", "sub", None),
        P("agg", "sub", None, None),
        P("agg", "sub", None),
        P("agg", "sub", None),
    )
    out_specs = (P("agg", "sub", None, None), P("agg", "sub", None, None))
    return jax.shard_map(shards, mesh=mesh, in_specs=in_specs, out_specs=out_specs, check_vma=False)
```

```python
import functools

import jax
import jax.numpy as jnp
from jax import lax
from jax.experimental import pallas as pl
from jax.experimental.pallas import tpu as pltpu
from jax.sharding import PartitionSpec as P

NB = 8
FMAX = 192
NI = 1536
NRHS = 64
NP = 128
NC = 1024
CAP = 48
N_SUB = 32
N_AGG = 8
WIDE = 4
BLOCKS = 5
N_DEV = N_SUB * N_AGG
HALF = 64
LANES = 128
PACKED = N_AGG * HALF
TILE = 256
HI = NC // LANES
DOT_RZ, DOT_OWN, DOT_CROSS, DOT_COARSE = CAP, CAP + 1, CAP + 2, CAP + 3
F32 = jnp.float32
BF16 = jnp.bfloat16
I32 = jnp.int32
LANES_BOTH = (((1,), (1,)), ((), ()))
VMEM = pl.BlockSpec(memory_space=pltpu.VMEM)
SMEM = pl.BlockSpec(memory_space=pltpu.SMEM)
FACE = jax.ShapeDtypeStruct((NRHS, FMAX), F32)
FIELD = jax.ShapeDtypeStruct((NRHS, NI), F32)


def direction_of(here, peer):
    turn = (peer - here) % WIDE
    same = peer // WIDE == here // WIDE
    step = jnp.where((peer - here) % N_SUB == WIDE, 6, 7)
    near = jnp.where(turn == 1, 4, 5)
    far = jnp.where(turn == 1, 2, 3)
    across = jnp.where(same, jnp.where(turn == 2, 1, near), jnp.where(turn == 2, 0, far))
    return jnp.where(turn == 0, step, across)


def move(index, direction):
    z, x = index // WIDE, index % WIDE
    if direction >= 6:
        return (z + (1 if direction == 6 else -1)) % (N_SUB // WIDE) * WIDE + x
    turn = (2, 2, 1, 3, 1, 3)[direction]
    target = (x + turn) % WIDE
    if direction in (0, 2, 3):
        z = (z + (1 if target < x else -1)) % (N_SUB // WIDE)
    return z * WIDE + target


def face_table(peers, counts):
    here = lax.axis_index("sub").astype(I32)
    leaves = jnp.where(peers < 0, NB, direction_of(here, peers))
    arrives = jnp.where(peers < 0, 0, direction_of(peers, here))
    return jnp.concatenate([leaves, arrives, counts])


def inside(table_ref, slot):
    depth = lax.broadcasted_iota(I32, (NRHS, FMAX), 1)
    return depth < table_ref[2 * NB + slot]


def face(slot):
    return slice(slot * FMAX, (slot + 1) * FMAX)


def send_faces(buffer, out_refs):
    for direction in range(NB):
        out_refs[direction][...] = buffer[direction]


def take_faces(buffer, in_refs):
    for direction in range(NB):
        buffer[direction] = in_refs[direction][...]


def assembled(local_ref, buffer, table_ref, slot):
    total = local_ref[:, face(slot)] + buffer[table_ref[NB + slot]]
    return jnp.where(inside(table_ref, slot), total, 0.0)


def row_sum(value):
    return jnp.sum(value, axis=1, keepdims=True)


def half_kernel(block_ref, rows_ref, held_ref):
    for ahead in range(BLOCKS):
        start = lax.rem(block_ref[0] + ahead, HI) * LANES
        held_ref[:, ahead * LANES : (ahead + 1) * LANES] = rows_ref[
            :, pl.ds(pl.multiple_of(start, LANES), LANES)
        ]


def load_kernel(table_ref, load_ref, *rest):
    outs, buffer = rest[:NB], rest[NB]
    for slot in range(NB):
        value = jnp.where(inside(table_ref, slot), load_ref[:, face(slot)], 0.0)
        buffer[table_ref[slot]] = value
    send_faces(buffer, outs)


def column(row):
    return jnp.broadcast_to(row, (NP, NP)).T


def packing_kernel(owner_ref, row_ref, coupling_ref, packed_ref, ids_ref):
    owner = owner_ref[...].astype(F32)
    down = lax.broadcasted_iota(I32, (NP, NP), 0)
    across = lax.broadcasted_iota(I32, (NP, NP), 1)
    earlier = (column(owner) == owner) & (down < across)
    place = owner * HALF + jnp.sum(jnp.where(earlier, 1.0, 0.0), axis=0, keepdims=True)
    packing = lax.broadcasted_iota(I32, (PACKED, NP), 0) == place.astype(I32)
    packed_ref[...] = jnp.dot(
        jnp.where(packing, 1.0, 0.0).astype(BF16), coupling_ref[...], preferred_element_type=F32
    ).astype(BF16)
    place_col = column(place)[:, :1].astype(I32)
    named = column(row_ref[...].astype(F32) + 1.0)[:, :1]
    hit = lax.broadcasted_iota(I32, (NP, PACKED), 1) == place_col
    ids_ref[...] = jnp.sum(jnp.where(hit, named, 0.0), axis=0, keepdims=True) - 1.0


def multiply(field_bf, matrix_ref, product_ref):
    for start in range(0, NI, TILE):
        product_ref[:, start : start + TILE] = jnp.dot(
            field_bf[...], matrix_ref[:, start : start + TILE], preferred_element_type=F32
        )


def smooth(field_bf, matrix_ref, table_ref, local_ref, buffer):
    multiply(field_bf, matrix_ref, local_ref)
    for slot in range(NB):
        value = jnp.where(inside(table_ref, slot), local_ref[:, face(slot)], 0.0)
        local_ref[:, face(slot)] = value
        buffer[table_ref[slot]] = value


def first_precond_kernel(table_ref, load_ref, matrix_ref, *rest):
    ins, outs = rest[:NB], rest[NB : 2 * NB]
    residual_ref, local_ref, buffer, field_bf = rest[2 * NB :]
    take_faces(buffer, ins)
    for slot in range(NB):
        value = assembled(load_ref, buffer, table_ref, slot)
        residual_ref[:, face(slot)] = value
        field_bf[:, face(slot)] = value.astype(BF16)
    smooth(field_bf, matrix_ref, table_ref, local_ref, buffer)
    send_faces(buffer, outs)


def next_precond_kernel(
    table_ref, image_ref, residual_in, scalars_ref, matrix_ref, *rest
):
    ins, outs = rest[:NB], rest[NB : 2 * NB]
    full_ref, residual_ref, local_ref, buffer, field_bf = rest[2 * NB :]
    take_faces(buffer, ins)
    alpha = scalars_ref[:, 0:1]
    for slot in range(NB):
        value = assembled(image_ref, buffer, table_ref, slot)
        full_ref[:, face(slot)] = value
        value = residual_in[:, face(slot)] - alpha * value
        residual_ref[:, face(slot)] = value
        field_bf[:, face(slot)] = value.astype(BF16)
    smooth(field_bf, matrix_ref, table_ref, local_ref, buffer)
    send_faces(buffer, outs)


def operator_kernel(first, table_ref, local_ref, residual_ref, *rest):
    rest = list(rest)
    image_ref = None if first else rest.pop(0)
    packed_ref, ids_ref, matrix_ref = rest[:3]
    ins = rest[3 : 3 + NB]
    field_ref, own_ref, send_ref, buffer, field_bf = rest[3 + NB :]
    take_faces(buffer, ins)
    for slot in range(NB):
        value = assembled(local_ref, buffer, table_ref, slot)
        field_ref[:, face(slot)] = value
        field_bf[:, face(slot)] = value.astype(BF16)
    terms = lax.dot_general(
        field_bf[...], packed_ref[...], LANES_BOTH, preferred_element_type=F32
    )
    multiply(field_bf, matrix_ref, own_ref)
    field = field_ref[...]
    rz = row_sum(residual_ref[...] * field)
    own_dot = row_sum(field * own_ref[...])
    place = lax.bitwise_and(lax.broadcasted_iota(I32, (NRHS, PACKED), 1), HALF - 1)
    terms = jnp.where(place == DOT_RZ, rz, terms)
    terms = jnp.where(place == DOT_OWN, own_dot, terms)
    if not first:
        terms = jnp.where(place == DOT_CROSS, row_sum(field * image_ref[...]), terms)
    for owner in range(N_AGG):
        piece = terms[:, owner * HALF : (owner + 1) * HALF]
        message = jnp.concatenate([piece[:N_SUB], piece[N_SUB:]], axis=1)
        if first:
            send_ref[pl.ds(2 * owner * N_SUB, N_SUB, stride=2), :] = message
            named = ids_ref[:, owner * HALF : (owner + 1) * HALF]
            named = jnp.broadcast_to(jnp.concatenate([named, named], axis=1), (N_SUB, LANES))
            send_ref[pl.ds(2 * owner * N_SUB + 1, N_SUB, stride=2), :] = named
        else:
            send_ref[owner * N_SUB : (owner + 1) * N_SUB, :] = message


def split3(value):
    high = value.astype(BF16).astype(F32)
    rest = value - high
    middle = rest.astype(BF16).astype(F32)
    return high, middle, rest - middle


def sources(j):
    return slice(j * N_DEV, (j + 1) * N_DEV)


def add_up_kernel(first, got_ref, *rest):
    if first:
        values_ref, rhs_ref, low_ref, high_ref = rest
        values_ref[...] = got_ref[pl.ds(0, N_DEV, stride=2), :].T
        named = got_ref[pl.ds(1, N_DEV, stride=2), :].T.astype(I32)[:HALF]
        high_ref[...] = lax.shift_right_arithmetic(named, 7)
        low_rows = lax.bitwise_and(named, LANES - 1)
        down = lax.broadcasted_iota(I32, (LANES, N_DEV), 0)
        for j in range(CAP):
            hit = down == low_rows[j : j + 1, :]
            low_ref[:, sources(j)] = jnp.where(hit, 1.0, 0.0).astype(BF16)
    else:
        low_ref, high_ref, values_ref, rhs_ref = rest
        values_ref[...] = got_ref[...].T
    parts = split3(values_ref[...])
    up = lax.broadcasted_iota(I32, (HI, N_DEV), 0)
    total = jnp.zeros((LANES, 6 * HI), F32)
    for j in range(CAP):
        hit = up == high_ref[j : j + 1, :]
        spread = [
            jnp.where(hit, part[case * HALF + j : case * HALF + j + 1, :], 0.0)
            for part in parts
            for case in range(2)
        ]
        total += lax.dot_general(
            low_ref[:, sources(j)],
            jnp.concatenate(spread, axis=0).astype(BF16),
            LANES_BOTH,
            preferred_element_type=F32,
        )
    width = 2 * HI
    rhs_ref[...] = total[:, :width] + total[:, width : 2 * width] + total[:, 2 * width :]


def solve_kernel(values_ref, rhs_ref, low_ref, high_ref, inverse_ref, send_ref, answer):
    width = 2 * HI
    rhs = rhs_ref[...]
    wide = jnp.concatenate([rhs, jnp.zeros((LANES, LANES - width), F32)], axis=1).T
    totals = jnp.broadcast_to(row_sum(values_ref[...]), (LANES, N_DEV))
    rows = []
    for case in range(2):
        total = [jnp.zeros((1, LANES), F32)] * HI
        for block in range(HI):
            held = inverse_ref[block * LANES : (block + 1) * LANES, :]
            at = case * HI + block
            below = jnp.sum(held * rhs[:, at : at + 1], axis=0, keepdims=True)
            across = jnp.zeros((LANES, LANES), F32)
            for ahead in range(BLOCKS):
                other = (block + ahead) % HI
                lanes = slice(ahead * LANES, (ahead + 1) * LANES)
                total[other] += below[:, lanes]
                if 0 < ahead < BLOCKS - 1:
                    row = case * HI + other
                    across += held[:, lanes] * wide[row : row + 1, :]
            total[block] += jnp.sum(across.T, axis=0, keepdims=True)
        rows += total
    stacked = jnp.concatenate(split3(jnp.concatenate(rows, axis=0)), axis=0).astype(BF16)
    up = lax.broadcasted_iota(I32, (HI, N_DEV), 0)
    for j in range(CAP):
        hit = up == high_ref[j : j + 1, :]
        picked = jnp.dot(stacked, low_ref[:, sources(j)], preferred_element_type=F32)
        picked = picked[:width] + picked[width : 2 * width] + picked[2 * width :]
        for case in range(2):
            mine = jnp.where(hit, picked[case * HI : (case + 1) * HI], 0.0)
            row = case * HALF + j
            answer[row : row + 1, :] = jnp.sum(mine, axis=0, keepdims=True)
    for case in range(2):
        rows = slice(case * HALF, case * HALF + CAP)
        spare = slice(case * HALF + CAP, (case + 1) * HALF)
        answer[spare, :] = totals[spare]
        both = row_sum(values_ref[rows, :] * answer[rows, :])
        both = jnp.broadcast_to(jnp.sum(both, axis=0, keepdims=True), (1, N_DEV))
        answer[case * HALF + DOT_COARSE : case * HALF + DOT_COARSE + 1, :] = both
    send_ref[...] = answer[...].T


def coarse_kernel(first, got_ref, inverse_ref, *rest):
    *rest, values, rhs, answer = rest
    if first:
        send_ref, low_ref, high_ref = rest
        add_up_kernel(first, got_ref, values, rhs, low_ref, high_ref)
    else:
        low_ref, high_ref, send_ref = rest
        add_up_kernel(first, got_ref, low_ref, high_ref, values, rhs)
    solve_kernel(values, rhs, low_ref, high_ref, inverse_ref, send_ref, answer)


def correct_kernel(first, table_ref, got_ref, packed_ref, own_ref, *rest):
    rest = list(rest)
    before_ref = None if first else rest.pop(0)
    local_ref, scalars_ref = rest[:2]
    outs = rest[2 : 2 + NB]
    buffer, back = rest[2 + NB :]
    for owner in range(N_AGG):
        block = got_ref[owner * N_SUB : (owner + 1) * N_SUB, :]
        back[:, owner * HALF : (owner + 1) * HALF] = jnp.concatenate(
            [block[:, :HALF], block[:, HALF:]], axis=0
        )
    correction = jnp.dot(back[...].astype(BF16), packed_ref[...], preferred_element_type=F32)
    for slot in range(NB):
        value = own_ref[:, face(slot)] + correction[:, face(slot)]
        value = jnp.where(inside(table_ref, slot), value, 0.0)
        local_ref[:, face(slot)] = value
        buffer[table_ref[slot]] = value
    send_faces(buffer, outs)
    coarse = back[:, DOT_COARSE : DOT_COARSE + 1]
    for owner in range(1, N_AGG):
        at = owner * HALF + DOT_COARSE
        coarse = coarse + back[:, at : at + 1]
    rz = back[:, DOT_RZ : DOT_RZ + 1]
    energy = 2.0 * (back[:, DOT_OWN : DOT_OWN + 1] + coarse)
    lane = lax.broadcasted_iota(I32, (NRHS, LANES), 1)
    if first:
        columns = (rz / energy, rz, energy)
    else:
        beta = rz / before_ref[:, 1:2]
        cross = back[:, DOT_CROSS : DOT_CROSS + 1]
        energy = energy + 2.0 * beta * cross + beta * beta * before_ref[:, 2:3]
        columns = (rz / energy, beta, before_ref[:, 0:1])
    scalars = jnp.zeros((NRHS, LANES), F32)
    for index, column in enumerate(columns):
        scalars = jnp.where(lane == index, column, scalars)
    scalars_ref[...] = scalars


def final_kernel(
    table_ref,
    local_ref,
    image_ref,
    residual_in,
    field0_ref,
    field1_ref,
    scalars_ref,
    *rest,
):
    ins = rest[:NB]
    solution_ref, residual_ref, buffer = rest[NB:]
    take_faces(buffer, ins)
    alpha, beta = scalars_ref[:, 0:1], scalars_ref[:, 1:2]
    alpha_before = scalars_ref[:, 2:3]
    for slot in range(NB):
        value = assembled(local_ref, buffer, table_ref, slot)
        value = value + beta * image_ref[:, face(slot)]
        residual_ref[:, face(slot)] = residual_in[:, face(slot)] - alpha * value
    before = field0_ref[...]
    solution_ref[...] = alpha_before * before + alpha * (field1_ref[...] + beta * before)


def exchange(blocks):
    moved = []
    for direction, block in enumerate(blocks):
        route = [(index, move(index, direction)) for index in range(N_SUB)]
        moved.append(lax.ppermute(block, "sub", route))
    return moved


FACES = pltpu.VMEM((NB + 1, NRHS, FMAX), F32)
PACKED_FIELD = pltpu.VMEM((NRHS, NI), BF16)


def call(kernel, outs, in_specs, scratch):
    return pl.pallas_call(
        kernel,
        out_shape=outs,
        in_specs=in_specs,
        out_specs=[VMEM] * len(outs),
        scratch_shapes=scratch,
        compiler_params=pltpu.CompilerParams(vmem_limit_bytes=24 << 20),
    )


def shards(
    dual_load,
    interface_inverse,
    dirichlet,
    coupling,
    neighbours,
    face_counts,
    owners,
    primal_rows,
    coarse_inverse,
):
    load = dual_load[0, 0]
    stiffness, dirichlet_block = interface_inverse[0, 0], dirichlet[0, 0]
    table = face_table(neighbours[0, 0], face_counts[0, 0])
    block = (lax.axis_index("sub") // (N_SUB // HI)).astype(I32)[None]
    (held,) = call(
        half_kernel,
        [jax.ShapeDtypeStruct((NC // N_SUB, BLOCKS * LANES), F32)],
        [SMEM, VMEM],
        [],
    )(block, coarse_inverse[0])
    inverse = lax.all_gather(held, "sub", axis=0, tiled=True)
    faces = call(load_kernel, [FACE] * NB, [SMEM, VMEM], [FACES])(table, load)
    packed, ids = call(
        packing_kernel,
        [jax.ShapeDtypeStruct((PACKED, NI), BF16), jax.ShapeDtypeStruct((1, PACKED), F32)],
        [VMEM] * 3,
        [],
    )(owners[0, 0].reshape(1, NP), primal_rows[0], coupling[0, 0])
    faces = exchange(faces)
    *faces, residual, local = call(
        first_precond_kernel,
        [FACE] * NB + [FIELD, FIELD],
        [SMEM] + [VMEM] * (2 + NB),
        [FACES, PACKED_FIELD],
    )(table, load, dirichlet_block, *faces)
    message = jax.ShapeDtypeStruct((N_DEV, LANES), F32)
    low_shape = jax.ShapeDtypeStruct((LANES, CAP * N_DEV), BF16)
    high_shape = jax.ShapeDtypeStruct((HALF, N_DEV), I32)
    axes = ("agg", "sub")
    low = high = scalars = image = field0 = None
    for step in range(2):
        first = step == 0
        faces = exchange(faces)
        extra = [] if first else [image]
        send_shape = jax.ShapeDtypeStruct((2 * N_DEV if first else N_DEV, LANES), F32)
        field, own, send = call(
            functools.partial(operator_kernel, first),
            [FIELD, FIELD, send_shape],
            [SMEM] + [VMEM] * (2 + len(extra)) + [VMEM] * (3 + NB),
            [FACES, PACKED_FIELD],
        )(table, local, residual, *extra, packed, ids, stiffness, *faces)
        pieces = 2 if first else 1
        got = lax.all_to_all(
            send.reshape(N_DEV, pieces, LANES), axes, split_axis=0, concat_axis=0, tiled=True
        ).reshape(N_DEV * pieces, LANES)
        answer, *names = call(
            functools.partial(coarse_kernel, first),
            [message, low_shape, high_shape] if first else [message],
            [VMEM] * (2 if first else 4),
            [
                pltpu.VMEM((LANES, N_DEV), F32),
                pltpu.VMEM((LANES, 2 * HI), F32),
                pltpu.VMEM((LANES, N_DEV), F32),
            ],
        )(got, inverse, *([] if first else [low, high]))
        if first:
            low, high = names
        got = lax.all_to_all(
            answer.reshape(N_DEV, 1, LANES), axes, split_axis=0, concat_axis=0, tiled=True
        ).reshape(N_DEV, LANES)
        extra = [] if first else [scalars]
        local, scalars, *faces = call(
            functools.partial(correct_kernel, first),
            [FIELD, jax.ShapeDtypeStruct((NRHS, LANES), F32)] + [FACE] * NB,
            [SMEM] + [VMEM] * (3 + len(extra)),
            [FACES, pltpu.VMEM((NRHS, PACKED), F32)],
        )(table, got, packed, own, *extra)
        faces = exchange(faces)
        if first:
            field0 = field
            *faces, image, residual, local = call(
                next_precond_kernel,
                [FACE] * NB + [FIELD] * 3,
                [SMEM] + [VMEM] * (4 + NB),
                [FACES, PACKED_FIELD],
            )(table, local, residual, scalars, dirichlet_block, *faces)
    solution_out, residual_out = call(
        final_kernel,
        [FIELD, FIELD],
        [SMEM] + [VMEM] * (6 + NB),
        [FACES],
    )(table, local, image, residual, field0, field, scalars, *faces)
    return (solution_out[None, None], residual_out[None, None])


def solution(mesh):
    in_specs = (
        P("agg", "sub", None, None),
        P("agg", "sub", None, None),
        P("agg", "sub", None, None),
        P("agg", "sub", None, None),
        P("agg", "sub", None),
        P("agg", "sub", None),
        P("agg", "sub", None, None),
        P("agg", "sub", None),
        P("agg", "sub", None),
    )
    out_specs = (P("agg", "sub", None, None), P("agg", "sub", None, None))
    return jax.shard_map(shards, mesh=mesh, in_specs=in_specs, out_specs=out_specs, check_vma=False)
```

```python
import functools

import jax
import jax.numpy as jnp
from jax import lax
from jax.experimental import pallas as pl
from jax.experimental.pallas import tpu as pltpu
from jax.sharding import PartitionSpec as P

NB = 8
FMAX = 192
NI = 1536
NRHS = 64
NP = 128
NC = 1024
CAP = 48
N_SUB = 32
N_AGG = 8
WIDE = 4
BLOCKS = 5
N_DEV = N_SUB * N_AGG
HALF = 64
LANES = 128
PACKED = N_AGG * HALF
TILE = 256
HI = NC // LANES
DOT_RZ, DOT_OWN, DOT_CROSS, DOT_COARSE = CAP, CAP + 1, CAP + 2, CAP + 3
F32 = jnp.float32
BF16 = jnp.bfloat16
I32 = jnp.int32
LANES_BOTH = (((1,), (1,)), ((), ()))
VMEM = pl.BlockSpec(memory_space=pltpu.VMEM)
SMEM = pl.BlockSpec(memory_space=pltpu.SMEM)
FACE = jax.ShapeDtypeStruct((NRHS, FMAX), F32)
FIELD = jax.ShapeDtypeStruct((NRHS, NI), F32)


def direction_of(here, peer):
    turn = (peer - here) % WIDE
    same = peer // WIDE == here // WIDE
    step = jnp.where((peer - here) % N_SUB == WIDE, 3, 5)
    near = jnp.where(turn == 1, 6, 7)
    far = jnp.where(turn == 1, 2, 4)
    across = jnp.where(same, jnp.where(turn == 2, 1, near), jnp.where(turn == 2, 0, far))
    return jnp.where(turn == 0, step, across)


def move(index, direction):
    z, x = index // WIDE, index % WIDE
    if direction in (3, 5):
        return (z + (1 if direction == 3 else -1)) % (N_SUB // WIDE) * WIDE + x
    turn = (2, 2, 1, 0, 3, 0, 1, 3)[direction]
    target = (x + turn) % WIDE
    if direction in (0, 2, 4):
        z = (z + (1 if target < x else -1)) % (N_SUB // WIDE)
    return z * WIDE + target


def face_table(peers, counts):
    here = lax.axis_index("sub").astype(I32)
    leaves = jnp.where(peers < 0, NB, direction_of(here, peers))
    arrives = jnp.where(peers < 0, 0, direction_of(peers, here))
    return jnp.concatenate([leaves, arrives, counts])


def inside(table_ref, slot):
    depth = lax.broadcasted_iota(I32, (NRHS, FMAX), 1)
    return depth < table_ref[2 * NB + slot]


def face(slot):
    return slice(slot * FMAX, (slot + 1) * FMAX)


def send_faces(buffer, out_refs):
    for direction in range(NB):
        out_refs[direction][...] = buffer[direction]


def take_faces(buffer, in_refs):
    for direction in range(NB):
        buffer[direction] = in_refs[direction][...]


def assembled(local_ref, buffer, table_ref, slot):
    total = local_ref[:, face(slot)] + buffer[table_ref[NB + slot]]
    return jnp.where(inside(table_ref, slot), total, 0.0)


def row_sum(value):
    return jnp.sum(value, axis=1, keepdims=True)


def half_kernel(block_ref, rows_ref, held_ref):
    for ahead in range(BLOCKS):
        start = lax.rem(block_ref[0] + ahead, HI) * LANES
        held_ref[:, ahead * LANES : (ahead + 1) * LANES] = rows_ref[
            :, pl.ds(pl.multiple_of(start, LANES), LANES)
        ]


def load_kernel(table_ref, load_ref, *rest):
    outs, buffer = rest[:NB], rest[NB]
    for slot in range(NB):
        value = jnp.where(inside(table_ref, slot), load_ref[:, face(slot)], 0.0)
        buffer[table_ref[slot]] = value
    send_faces(buffer, outs)


def column(row):
    return jnp.broadcast_to(row, (NP, NP)).T


def packing_kernel(owner_ref, row_ref, coupling_ref, packed_ref, ids_ref):
    owner = owner_ref[...].astype(F32)
    down = lax.broadcasted_iota(I32, (NP, NP), 0)
    across = lax.broadcasted_iota(I32, (NP, NP), 1)
    earlier = (column(owner) == owner) & (down < across)
    place = owner * HALF + jnp.sum(jnp.where(earlier, 1.0, 0.0), axis=0, keepdims=True)
    packing = lax.broadcasted_iota(I32, (PACKED, NP), 0) == place.astype(I32)
    packed_ref[...] = jnp.dot(
        jnp.where(packing, 1.0, 0.0).astype(BF16), coupling_ref[...], preferred_element_type=F32
    ).astype(BF16)
    place_col = column(place)[:, :1].astype(I32)
    named = column(row_ref[...].astype(F32) + 1.0)[:, :1]
    hit = lax.broadcasted_iota(I32, (NP, PACKED), 1) == place_col
    ids_ref[...] = jnp.sum(jnp.where(hit, named, 0.0), axis=0, keepdims=True) - 1.0


def multiply(field_bf, matrix_ref, product_ref):
    for start in range(0, NI, TILE):
        product_ref[:, start : start + TILE] = jnp.dot(
            field_bf[...], matrix_ref[:, start : start + TILE], preferred_element_type=F32
        )


def smooth(field_bf, matrix_ref, table_ref, local_ref, buffer):
    multiply(field_bf, matrix_ref, local_ref)
    for slot in range(NB):
        value = jnp.where(inside(table_ref, slot), local_ref[:, face(slot)], 0.0)
        local_ref[:, face(slot)] = value
        buffer[table_ref[slot]] = value


def first_precond_kernel(table_ref, load_ref, matrix_ref, *rest):
    ins, outs = rest[:NB], rest[NB : 2 * NB]
    residual_ref, local_ref, buffer, field_bf = rest[2 * NB :]
    take_faces(buffer, ins)
    for slot in range(NB):
        value = assembled(load_ref, buffer, table_ref, slot)
        residual_ref[:, face(slot)] = value
        field_bf[:, face(slot)] = value.astype(BF16)
    smooth(field_bf, matrix_ref, table_ref, local_ref, buffer)
    send_faces(buffer, outs)


def next_precond_kernel(
    table_ref, image_ref, residual_in, scalars_ref, matrix_ref, *rest
):
    ins, outs = rest[:NB], rest[NB : 2 * NB]
    full_ref, residual_ref, local_ref, buffer, field_bf = rest[2 * NB :]
    take_faces(buffer, ins)
    alpha = scalars_ref[:, 0:1]
    for slot in range(NB):
        value = assembled(image_ref, buffer, table_ref, slot)
        full_ref[:, face(slot)] = value
        value = residual_in[:, face(slot)] - alpha * value
        residual_ref[:, face(slot)] = value
        field_bf[:, face(slot)] = value.astype(BF16)
    smooth(field_bf, matrix_ref, table_ref, local_ref, buffer)
    send_faces(buffer, outs)


def operator_kernel(first, table_ref, local_ref, residual_ref, *rest):
    rest = list(rest)
    image_ref = None if first else rest.pop(0)
    packed_ref, ids_ref, matrix_ref = rest[:3]
    ins = rest[3 : 3 + NB]
    field_ref, own_ref, send_ref, buffer, field_bf = rest[3 + NB :]
    take_faces(buffer, ins)
    for slot in range(NB):
        value = assembled(local_ref, buffer, table_ref, slot)
        field_ref[:, face(slot)] = value
        field_bf[:, face(slot)] = value.astype(BF16)
    terms = lax.dot_general(
        field_bf[...], packed_ref[...], LANES_BOTH, preferred_element_type=F32
    )
    multiply(field_bf, matrix_ref, own_ref)
    field = field_ref[...]
    rz = row_sum(residual_ref[...] * field)
    own_dot = row_sum(field * own_ref[...])
    place = lax.bitwise_and(lax.broadcasted_iota(I32, (NRHS, PACKED), 1), HALF - 1)
    terms = jnp.where(place == DOT_RZ, rz, terms)
    terms = jnp.where(place == DOT_OWN, own_dot, terms)
    if not first:
        terms = jnp.where(place == DOT_CROSS, row_sum(field * image_ref[...]), terms)
    for owner in range(N_AGG):
        piece = terms[:, owner * HALF : (owner + 1) * HALF]
        message = jnp.concatenate([piece[:N_SUB], piece[N_SUB:]], axis=1)
        if first:
            send_ref[pl.ds(2 * owner * N_SUB, N_SUB, stride=2), :] = message
            named = ids_ref[:, owner * HALF : (owner + 1) * HALF]
            named = jnp.broadcast_to(jnp.concatenate([named, named], axis=1), (N_SUB, LANES))
            send_ref[pl.ds(2 * owner * N_SUB + 1, N_SUB, stride=2), :] = named
        else:
            send_ref[owner * N_SUB : (owner + 1) * N_SUB, :] = message


def split3(value):
    high = value.astype(BF16).astype(F32)
    rest = value - high
    middle = rest.astype(BF16).astype(F32)
    return high, middle, rest - middle


def sources(j):
    return slice(j * N_DEV, (j + 1) * N_DEV)


def add_up_kernel(first, got_ref, *rest):
    if first:
        values_ref, rhs_ref, low_ref, high_ref = rest
        values_ref[...] = got_ref[pl.ds(0, N_DEV, stride=2), :].T
        named = got_ref[pl.ds(1, N_DEV, stride=2), :].T.astype(I32)[:HALF]
        high_ref[...] = lax.shift_right_arithmetic(named, 7)
        low_rows = lax.bitwise_and(named, LANES - 1)
        down = lax.broadcasted_iota(I32, (LANES, N_DEV), 0)
        for j in range(CAP):
            hit = down == low_rows[j : j + 1, :]
            low_ref[:, sources(j)] = jnp.where(hit, 1.0, 0.0).astype(BF16)
    else:
        low_ref, high_ref, values_ref, rhs_ref = rest
        values_ref[...] = got_ref[...].T
    parts = split3(values_ref[...])
    up = lax.broadcasted_iota(I32, (HI, N_DEV), 0)
    total = jnp.zeros((LANES, 6 * HI), F32)
    for j in range(CAP):
        hit = up == high_ref[j : j + 1, :]
        spread = [
            jnp.where(hit, part[case * HALF + j : case * HALF + j + 1, :], 0.0)
            for part in parts
            for case in range(2)
        ]
        total += lax.dot_general(
            low_ref[:, sources(j)],
            jnp.concatenate(spread, axis=0).astype(BF16),
            LANES_BOTH,
            preferred_element_type=F32,
        )
    width = 2 * HI
    rhs_ref[...] = total[:, :width] + total[:, width : 2 * width] + total[:, 2 * width :]


def solve_kernel(values_ref, rhs_ref, low_ref, high_ref, inverse_ref, send_ref, answer):
    width = 2 * HI
    rhs = rhs_ref[...]
    wide = jnp.concatenate([rhs, jnp.zeros((LANES, LANES - width), F32)], axis=1).T
    totals = jnp.broadcast_to(row_sum(values_ref[...]), (LANES, N_DEV))
    rows = []
    for case in range(2):
        total = [jnp.zeros((1, LANES), F32)] * HI
        for block in range(HI):
            held = inverse_ref[block * LANES : (block + 1) * LANES, :]
            at = case * HI + block
            below = jnp.sum(held * rhs[:, at : at + 1], axis=0, keepdims=True)
            across = jnp.zeros((LANES, LANES), F32)
            for ahead in range(BLOCKS):
                other = (block + ahead) % HI
                lanes = slice(ahead * LANES, (ahead + 1) * LANES)
                total[other] += below[:, lanes]
                if 0 < ahead < BLOCKS - 1:
                    row = case * HI + other
                    across += held[:, lanes] * wide[row : row + 1, :]
            total[block] += jnp.sum(across.T, axis=0, keepdims=True)
        rows += total
    stacked = jnp.concatenate(split3(jnp.concatenate(rows, axis=0)), axis=0).astype(BF16)
    up = lax.broadcasted_iota(I32, (HI, N_DEV), 0)
    for j in range(CAP):
        hit = up == high_ref[j : j + 1, :]
        picked = jnp.dot(stacked, low_ref[:, sources(j)], preferred_element_type=F32)
        picked = picked[:width] + picked[width : 2 * width] + picked[2 * width :]
        for case in range(2):
            mine = jnp.where(hit, picked[case * HI : (case + 1) * HI], 0.0)
            row = case * HALF + j
            answer[row : row + 1, :] = jnp.sum(mine, axis=0, keepdims=True)
    for case in range(2):
        rows = slice(case * HALF, case * HALF + CAP)
        spare = slice(case * HALF + CAP, (case + 1) * HALF)
        answer[spare, :] = totals[spare]
        both = row_sum(values_ref[rows, :] * answer[rows, :])
        both = jnp.broadcast_to(jnp.sum(both, axis=0, keepdims=True), (1, N_DEV))
        answer[case * HALF + DOT_COARSE : case * HALF + DOT_COARSE + 1, :] = both
    send_ref[...] = answer[...].T


def coarse_kernel(first, got_ref, inverse_ref, *rest):
    *rest, values, rhs, answer = rest
    if first:
        send_ref, low_ref, high_ref = rest
        add_up_kernel(first, got_ref, values, rhs, low_ref, high_ref)
    else:
        low_ref, high_ref, send_ref = rest
        add_up_kernel(first, got_ref, low_ref, high_ref, values, rhs)
    solve_kernel(values, rhs, low_ref, high_ref, inverse_ref, send_ref, answer)


def correct_kernel(first, table_ref, got_ref, packed_ref, own_ref, *rest):
    rest = list(rest)
    before_ref = None if first else rest.pop(0)
    local_ref, scalars_ref = rest[:2]
    outs = rest[2 : 2 + NB]
    buffer, back = rest[2 + NB :]
    for owner in range(N_AGG):
        block = got_ref[owner * N_SUB : (owner + 1) * N_SUB, :]
        back[:, owner * HALF : (owner + 1) * HALF] = jnp.concatenate(
            [block[:, :HALF], block[:, HALF:]], axis=0
        )
    correction = jnp.dot(back[...].astype(BF16), packed_ref[...], preferred_element_type=F32)
    for slot in range(NB):
        value = own_ref[:, face(slot)] + correction[:, face(slot)]
        value = jnp.where(inside(table_ref, slot), value, 0.0)
        local_ref[:, face(slot)] = value
        buffer[table_ref[slot]] = value
    send_faces(buffer, outs)
    coarse = back[:, DOT_COARSE : DOT_COARSE + 1]
    for owner in range(1, N_AGG):
        at = owner * HALF + DOT_COARSE
        coarse = coarse + back[:, at : at + 1]
    rz = back[:, DOT_RZ : DOT_RZ + 1]
    energy = 2.0 * (back[:, DOT_OWN : DOT_OWN + 1] + coarse)
    lane = lax.broadcasted_iota(I32, (NRHS, LANES), 1)
    if first:
        columns = (rz / energy, rz, energy)
    else:
        beta = rz / before_ref[:, 1:2]
        cross = back[:, DOT_CROSS : DOT_CROSS + 1]
        energy = energy + 2.0 * beta * cross + beta * beta * before_ref[:, 2:3]
        columns = (rz / energy, beta, before_ref[:, 0:1])
    scalars = jnp.zeros((NRHS, LANES), F32)
    for index, column in enumerate(columns):
        scalars = jnp.where(lane == index, column, scalars)
    scalars_ref[...] = scalars


def final_kernel(
    table_ref,
    local_ref,
    image_ref,
    residual_in,
    field0_ref,
    field1_ref,
    scalars_ref,
    *rest,
):
    ins = rest[:NB]
    solution_ref, residual_ref, buffer = rest[NB:]
    take_faces(buffer, ins)
    alpha, beta = scalars_ref[:, 0:1], scalars_ref[:, 1:2]
    alpha_before = scalars_ref[:, 2:3]
    for slot in range(NB):
        value = assembled(local_ref, buffer, table_ref, slot)
        value = value + beta * image_ref[:, face(slot)]
        residual_ref[:, face(slot)] = residual_in[:, face(slot)] - alpha * value
    before = field0_ref[...]
    solution_ref[...] = alpha_before * before + alpha * (field1_ref[...] + beta * before)


def exchange(blocks):
    moved = []
    for direction, block in enumerate(blocks):
        route = [(index, move(index, direction)) for index in range(N_SUB)]
        moved.append(lax.ppermute(block, "sub", route))
    return moved


FACES = pltpu.VMEM((NB + 1, NRHS, FMAX), F32)
PACKED_FIELD = pltpu.VMEM((NRHS, NI), BF16)


def call(kernel, outs, in_specs, scratch):
    return pl.pallas_call(
        kernel,
        out_shape=outs,
        in_specs=in_specs,
        out_specs=[VMEM] * len(outs),
        scratch_shapes=scratch,
        compiler_params=pltpu.CompilerParams(vmem_limit_bytes=24 << 20),
    )


def shards(
    dual_load,
    interface_inverse,
    dirichlet,
    coupling,
    neighbours,
    face_counts,
    owners,
    primal_rows,
    coarse_inverse,
):
    load = dual_load[0, 0]
    stiffness, dirichlet_block = interface_inverse[0, 0], dirichlet[0, 0]
    table = face_table(neighbours[0, 0], face_counts[0, 0])
    block = (lax.axis_index("sub") // (N_SUB // HI)).astype(I32)[None]
    (held,) = call(
        half_kernel,
        [jax.ShapeDtypeStruct((NC // N_SUB, BLOCKS * LANES), F32)],
        [SMEM, VMEM],
        [],
    )(block, coarse_inverse[0])
    inverse = lax.all_gather(held, "sub", axis=0, tiled=True)
    faces = call(load_kernel, [FACE] * NB, [SMEM, VMEM], [FACES])(table, load)
    packed, ids = call(
        packing_kernel,
        [jax.ShapeDtypeStruct((PACKED, NI), BF16), jax.ShapeDtypeStruct((1, PACKED), F32)],
        [VMEM] * 3,
        [],
    )(owners[0, 0].reshape(1, NP), primal_rows[0], coupling[0, 0])
    faces = exchange(faces)
    *faces, residual, local = call(
        first_precond_kernel,
        [FACE] * NB + [FIELD, FIELD],
        [SMEM] + [VMEM] * (2 + NB),
        [FACES, PACKED_FIELD],
    )(table, load, dirichlet_block, *faces)
    message = jax.ShapeDtypeStruct((N_DEV, LANES), F32)
    low_shape = jax.ShapeDtypeStruct((LANES, CAP * N_DEV), BF16)
    high_shape = jax.ShapeDtypeStruct((HALF, N_DEV), I32)
    axes = ("agg", "sub")
    low = high = scalars = image = field0 = None
    for step in range(2):
        first = step == 0
        faces = exchange(faces)
        extra = [] if first else [image]
        send_shape = jax.ShapeDtypeStruct((2 * N_DEV if first else N_DEV, LANES), F32)
        field, own, send = call(
            functools.partial(operator_kernel, first),
            [FIELD, FIELD, send_shape],
            [SMEM] + [VMEM] * (2 + len(extra)) + [VMEM] * (3 + NB),
            [FACES, PACKED_FIELD],
        )(table, local, residual, *extra, packed, ids, stiffness, *faces)
        pieces = 2 if first else 1
        got = lax.all_to_all(
            send.reshape(N_DEV, pieces, LANES), axes, split_axis=0, concat_axis=0, tiled=True
        ).reshape(N_DEV * pieces, LANES)
        answer, *names = call(
            functools.partial(coarse_kernel, first),
            [message, low_shape, high_shape] if first else [message],
            [VMEM] * (2 if first else 4),
            [
                pltpu.VMEM((LANES, N_DEV), F32),
                pltpu.VMEM((LANES, 2 * HI), F32),
                pltpu.VMEM((LANES, N_DEV), F32),
            ],
        )(got, inverse, *([] if first else [low, high]))
        if first:
            low, high = names
        got = lax.all_to_all(
            answer.reshape(N_DEV, 1, LANES), axes, split_axis=0, concat_axis=0, tiled=True
        ).reshape(N_DEV, LANES)
        extra = [] if first else [scalars]
        local, scalars, *faces = call(
            functools.partial(correct_kernel, first),
            [FIELD, jax.ShapeDtypeStruct((NRHS, LANES), F32)] + [FACE] * NB,
            [SMEM] + [VMEM] * (3 + len(extra)),
            [FACES, pltpu.VMEM((NRHS, PACKED), F32)],
        )(table, got, packed, own, *extra)
        faces = exchange(faces)
        if first:
            field0 = field
            *faces, image, residual, local = call(
                next_precond_kernel,
                [FACE] * NB + [FIELD] * 3,
                [SMEM] + [VMEM] * (4 + NB),
                [FACES, PACKED_FIELD],
            )(table, local, residual, scalars, dirichlet_block, *faces)
    solution_out, residual_out = call(
        final_kernel,
        [FIELD, FIELD],
        [SMEM] + [VMEM] * (6 + NB),
        [FACES],
    )(table, local, image, residual, field0, field, scalars, *faces)
    return (solution_out[None, None], residual_out[None, None])


def solution(mesh):
    in_specs = (
        P("agg", "sub", None, None),
        P("agg", "sub", None, None),
        P("agg", "sub", None, None),
        P("agg", "sub", None, None),
        P("agg", "sub", None),
        P("agg", "sub", None),
        P("agg", "sub", None, None),
        P("agg", "sub", None),
        P("agg", "sub", None),
    )
    out_specs = (P("agg", "sub", None, None), P("agg", "sub", None, None))
    return jax.shard_map(shards, mesh=mesh, in_specs=in_specs, out_specs=out_specs, check_vma=False)
```
